256 devices in a mesh: cells: 16 (over z, core), lev: 16 (over x, y).
Axes of the slice: x: 4, y: 4, z: 8, core: 2. Of those that a mesh axis runs over, the one named last changes fastest.
Arguments:
- source_levels: float32 [128, 65536], P('lev', 'cells'), may hold values from -6 to 6
- level_to_mode: float32 [128, 128], replicated, may hold values from -0.5 to 0.5
- mode_to_level: float32 [128, 128], replicated, may hold values from -0.5 to 0.5
- mode_shift: float32 [128], P('lev'), may hold values from 0.02 to 1
- edge_weight: float32 [6, 65536], P(None, 'cells'), may hold values from 0.05 to 0.5
- neighbours: int32 [6, 65536], P(None, 'cells'), may hold values from 0 to 6143, as said below
- send_lists: int32 [16, 2048], P('cells'), may hold values from 0 to 4095, as said below
Outputs:
- correction: float32 [128, 65536], P('lev', 'cells')
The draws below stay inside these ranges and needn't reach their ends.
Inputs may be any that keep to these rules, and one draw needn't show every extreme that they name: `neighbours`: an entry below 4096 is a cell of the same partition whose local index differs from the cell's own local index by at most 32; an entry e of partition p at or above 4096 names halo slot h = (e - 4096) % 128 from partition s = (e - 4096) // 128, with s not p and h below the number of cells that s sends to p. An unused entry names the cell itself. `send_lists`: the number of used slots from partition s to partition q differs from pair to pair: 1 to 128 for every pair of different partitions, 0 for a partition and itself; in every draw some partition receives 128 cells from every other one. Unused slots hold any cell.
All inputs are finite; a program needn't handle non-finite values.
Results may differ from the reference program's by a relative error of at most 0.00007.
Values sent between devices are 32-bit elements; how exact they have to be, the bound alone decides.
A program may use at most 64 MiB of HBM per device.

```python
import math
import jax
import jax.numpy as jnp
from jax import lax

L = 128
C_DEV = 4096
DEG = 6
HMAX = 128
SWEEPS = 2
STEPS = 4
NPART = 16
NCELLS = 65536


def halo_counts(key):
    key_counts, key_full = jax.random.split(jax.random.fold_in(key, 11))
    counts = jax.random.randint(key_counts, (NPART, NPART), 1, HMAX + 1)
    full_receiver = jax.random.randint(key_full, (), 0, NPART - 1)
    receiver = jnp.arange(NPART)[None, :]
    counts = jnp.where(receiver == full_receiver, HMAX, counts)
    counts = jnp.where(jnp.eye(NPART, dtype=bool), 0, counts)
    return (counts.astype(jnp.int32), full_receiver)


def draw_neighbours(key, part):
    counts, full_receiver = halo_counts(key)
    subkeys = jax.random.split(jax.random.fold_in(key, 23), 6)
    all_cells = C_DEV * NPART
    grid_shape = (DEG, all_cells)
    cell_index = jnp.arange(all_cells, dtype=jnp.int32)
    cell_owner = cell_index // C_DEV
    inner_index = cell_index % C_DEV
    step_size = jax.random.randint(subkeys[0], grid_shape, 1, 33)
    direction_sign = jax.random.randint(subkeys[1], grid_shape, 0, 2) * 2 - 1
    forward_cell = inner_index[None, :] + direction_sign * step_size
    outside = (forward_cell < 0) | (forward_cell >= C_DEV)
    local_cell = jnp.where(outside, inner_index[None, :] - direction_sign * step_size, forward_cell)
    offset = jax.random.randint(subkeys[2], grid_shape, 1, NPART)
    source = (cell_owner[None, :] + offset) % NPART
    owner_grid = jnp.broadcast_to(cell_owner[None, :], grid_shape)
    live_count = counts[source, owner_grid]
    slot_index = jax.random.randint(subkeys[3], grid_shape, 0, live_count)
    halo_cells = C_DEV + source * HMAX + slot_index
    halo_pick = jax.random.randint(subkeys[4], grid_shape, 0, 16) == 0
    entries = jnp.where(halo_pick, halo_cells, local_cell)
    padded = jax.random.randint(subkeys[5], (all_cells,), 0, 8) == 0
    row_index = jnp.arange(DEG)[:, None]
    entries = jnp.where((row_index == DEG - 1) & padded[None, :], inner_index[None, :], entries)
    entries = entries.at[0, full_receiver * C_DEV].set(C_DEV + (NPART - 1) * HMAX + HMAX - 1)
    return entries.astype(jnp.int32)


def draw_send_lists(key, part):
    send_cells = jax.random.randint(jax.random.fold_in(key, 37), (NPART, NPART * HMAX), 0, C_DEV)
    send_cells = send_cells.at[0, NPART * HMAX - 1].set(C_DEV - 1)
    return send_cells.astype(jnp.int32)


def levels(own_key, shape, shards, low, top_value):
    loudness, own = 1.0, jax.random.fold_in(own_key, 6)
    for axis_at, shards_of in shards:
        steps = jnp.exp(jax.random.uniform(jax.random.fold_in(own, axis_at), (shards_of,), jnp.float32, low / len(shards), top_value / len(shards)))
        loudness = loudness * jnp.repeat(steps, shape[axis_at] // shards_of).reshape([-1 if axis == axis_at else 1 for axis in range(len(shape))])
    return loudness


def gaussian(key, dims, width, limit, pieces=(), kind=jnp.bfloat16):
    result = jax.random.normal(key, dims, jnp.float32) * width
    if len(pieces) > 0:
        result = levels(key, dims, pieces, -0.22, 0.18) * result
    return jnp.clip(result, min=-limit, max=limit).astype(kind)


def setup_inputs(seed: int = 0) -> dict:
    splits = jax.random.split(jax.random.key(seed), 8)
    return {
        "source_levels": gaussian(splits[0], (L, NCELLS), 1.0, 6.0, ((0, 16), (1, 16)), jnp.float32),
        "level_to_mode": gaussian(splits[1], (L, L), L ** -0.5, 0.5, (), jnp.float32),
        "mode_to_level": gaussian(splits[2], (L, L), L ** -0.5, 0.5, (), jnp.float32),
        "mode_shift": jnp.clip(jnp.exp(math.log(1.0) - 3.912023 * jax.random.uniform(splits[3], (L,), jnp.float32) ** levels(splits[3], (L,), ((0, 16),), -0.2, 0.2)), 0.02, 1.0),
        "edge_weight": jnp.clip(0.05 + 0.45 * jax.random.uniform(splits[4], (DEG, NCELLS), jnp.float32) ** levels(splits[4], (DEG, NCELLS), ((1, 16),), -0.2, 0.2), 0.05, 0.5),
        "neighbours": draw_neighbours(jax.random.fold_in(splits[7], 71), 0),
        "send_lists": draw_send_lists(jax.random.fold_in(splits[7], 71), 0),
    }


def global_neighbours(neighbours, send_lists):
    cell_index = jnp.arange(NCELLS, dtype=jnp.int32)
    cell_owner = (cell_index // C_DEV)[None, :]
    is_local = neighbours < C_DEV
    slot_index = jnp.maximum(neighbours - C_DEV, 0).astype(jnp.int32)
    source = (slot_index // HMAX).astype(jnp.int32)
    column = (cell_owner * HMAX + slot_index % HMAX).astype(jnp.int32)
    remote = source * C_DEV + send_lists[source, column]
    return jnp.where(is_local, cell_owner * C_DEV + neighbours, remote).astype(jnp.int32)


def apply_operator(field, shift_col, diagonal, edge_weight, global_ids):
    running = (shift_col + diagonal[None, :]) * field
    for slot_number in range(DEG):
        running = running - edge_weight[slot_number][None, :] * jnp.take(field, global_ids[slot_number], axis=1)
    return running


def reference(source_levels, level_to_mode, mode_to_level, mode_shift, edge_weight, neighbours, send_lists):
    global_ids = global_neighbours(neighbours, send_lists)
    diagonal = jnp.sum(edge_weight, axis=0)
    mode_field = jnp.dot(level_to_mode, source_levels, precision=lax.Precision.HIGHEST, preferred_element_type=jnp.float32)
    shift_col = mode_shift[:, None]
    radius = DEG / 2.0
    centre = shift_col + radius
    sigma_ratio = centre / radius
    answer = jnp.zeros_like(mode_field)
    remain = mode_field
    direction = jnp.zeros_like(mode_field)
    factor = 1.0 / sigma_ratio
    for sweep_index in range(SWEEPS):
        for step_index in range(STEPS):
            if step_index == 0:
                if sweep_index > 0:
                    remain = remain - apply_operator(direction, shift_col, diagonal, edge_weight, global_ids)
                factor = 1.0 / sigma_ratio
                direction = remain / centre
            else:
                remain = remain - apply_operator(direction, shift_col, diagonal, edge_weight, global_ids)
                newer = 1.0 / (2.0 * sigma_ratio - factor)
                direction = newer * factor * direction + (2.0 * newer / radius) * remain
                factor = newer
            answer = answer + direction
    return jnp.dot(mode_to_level, answer, precision=lax.Precision.HIGHEST, preferred_element_type=jnp.float32)
```

```python
import functools
import math

import jax
import jax.numpy as jnp
from jax import lax
from jax.experimental import pallas as pl
from jax.experimental.pallas import tpu as pltpu
from jax.sharding import PartitionSpec as P

DEG = 6
HMAX = 128
SWEEPS = 2
STEPS = 4
TERMS = SWEEPS * STEPS
RADIUS = DEG / 2.0
MESH = pl.DeviceIdType.MESH
GATHER = lax.GatherDimensionNumbers(
    offset_dims=(),
    collapsed_slice_dims=(1,),
    start_index_map=(1,),
    operand_batching_dims=(0,),
    start_indices_batching_dims=(0,),
)


def lane_gather(block, lanes):
    return lax.gather(
        block, lanes[..., None], GATHER, slice_sizes=(1, 1), mode=lax.GatherScatterMode.PROMISE_IN_BOUNDS
    )


def full_product(left, right):
    return jnp.dot(left, right, precision=lax.Precision.HIGHEST, preferred_element_type=jnp.float32)


def peers_of(chips):
    places, groups = [(0, 1)], [(0, 1)]
    for far in range(1, chips // 2 + 1):
        start = len(places)
        for step in sorted({far, chips - far}):
            places += [(step, 0), (step, 1)]
        groups.append((start, len(places)))
    return places, groups


def block(row):
    return jnp.broadcast_to(row, (8, 128))


def chebyshev_coefficients(shift):
    lane = lax.broadcasted_iota(jnp.int32, (8, 128), 1)
    up = jnp.where(lane == 0, 0.0, jnp.where(lane == 1, 1.0, 0.5))
    down = jnp.where(lane < TERMS, 0.5, 0.0)

    def operator(poly):
        scaled = up * pltpu.roll(poly, 1, 1) + down * pltpu.roll(poly, 127, 1)
        return centre * poly + RADIUS * scaled

    centre = shift + RADIUS
    sigma = centre / RADIUS
    answer = jnp.zeros((8, 128), jnp.float32)
    remain = jnp.where(lane == 0, 1.0, 0.0)
    direction = answer
    factor = 1.0 / sigma
    for sweep_index in range(SWEEPS):
        for step_index in range(STEPS):
            if sweep_index + step_index > 0:
                remain = remain - operator(direction)
            if step_index == 0:
                factor = 1.0 / sigma
                direction = remain / centre
            else:
                newer = 1.0 / (2.0 * sigma - factor)
                direction = newer * factor * direction + (2.0 * newer / RADIUS) * remain
                factor = newer
            answer = answer + direction
    return answer


def kernel(
    parts, slabs, group_rows, rounds_of,
    shift_ref, source_ref, l2m_ref, m2l_ref, weight_ref, near_ref, list_ref,
    out_ref, flag_ref,
    edge, weight, lane_a, weight_a, weight_b, own, halo_lane, halo_weight, pack,
    give_s, have_s, give_g, have_g, field, total, send, halo, flag_out, flag_in,
    sem_s, sem_g, sem_send, sem_recv, sem_flag,
):
    columns = source_ref.shape[1]
    tiles = columns // 128
    eighths = tiles // 8
    share = tiles // slabs
    part = lax.axis_index("cells")
    slab = lax.axis_index("lev")
    chips = parts // 2
    places, groups = peers_of(chips)
    count = len(places)
    chip, core = part // 2, part % 2
    inverse = [places.index(((chips - step) % chips, swap)) for step, swap in places]

    def partition_at(place):
        step, swap = places[place]
        return ((chip + step) % chips) * 2 + (core + swap) % 2

    barrier = pltpu.get_barrier_semaphore()
    for place in range(count):
        pl.semaphore_signal(barrier, inc=1, device_id={"cells": partition_at(place)}, device_id_type=MESH)
    for step in range(1, slabs):
        pl.semaphore_signal(barrier, inc=1, device_id={"lev": (slab + step) % slabs}, device_id_type=MESH)

    row = lax.broadcasted_iota(jnp.int32, (8, 128), 0)
    shift = jnp.zeros((8, 128), jnp.float32)
    for index in range(8):
        shift = jnp.where(row == index, shift_ref[index], shift)
    coefficients = chebyshev_coefficients(shift)
    for peer in range(slabs):
        for piece in range(share):
            at = (peer * share + piece) * 128
            give_s[peer, piece] = source_ref[:, at : at + 128]
        give_s[peer, share] = coefficients
    have_s[slab] = give_s[slab]

    pl.semaphore_wait(barrier, count + slabs - 1)

    order = sorted(range(1, slabs), key=lambda step: -(step * 7 % slabs))
    for step in order:
        peer = (slab + step) % slabs
        pltpu.make_async_remote_copy(
            src_ref=give_s.at[peer], dst_ref=have_s.at[slab], send_sem=sem_s.at[0], recv_sem=sem_s.at[1],
            device_id={"lev": peer}, device_id_type=MESH,
        ).start()

    for k in range(DEG):
        for tile in range(tiles):
            edge[k, tile // 8, tile % 8 : tile % 8 + 1, :] = near_ref[k : k + 1, tile * 128 : tile * 128 + 128]
            weight[k, tile // 8, tile % 8 : tile % 8 + 1, :] = weight_ref[k : k + 1, tile * 128 : tile * 128 + 128]
    for g in range(eighths):
        diagonal = jnp.zeros((8, 128), jnp.float32)
        for k in range(DEG):
            entry = edge[k, g]
            value = weight[k, g]
            diagonal = diagonal + value
            scaled = value * (-2.0 / RADIUS)
            inside = entry < columns
            here = (entry >> 7) == (row + 8 * g)
            lane_a[k, g] = entry & 127
            weight_a[k, g] = jnp.where(here, scaled, 0.0)
            weight_b[k, g] = jnp.where(inside, jnp.where(here, 0.0, scaled), 0.0)
            edge[k, g] = jnp.where(inside, -1, entry - columns)
            weight[k, g] = scaled
        own[g] = (diagonal - RADIUS) * (2.0 / RADIUS)
    for place in range(count):
        start = pl.multiple_of(partition_at(place) * HMAX, HMAX)
        pack[place] = block(list_ref[0:1, pl.ds(start, HMAX)])

    group_count = eighths // group_rows

    def build(place, most):
        pair = (place + 1) // 2
        step = jnp.where(pair % 2 == 1, (pair + 1) // 2, chips - pair // 2)
        step = jnp.where(pair == 0, 0, step)
        wanted = ((chip + step) % chips) * 2 + (core + (place + 1) % 2) % 2
        for group in range(group_count):
            seen = jnp.zeros((8, 128), jnp.int32)
            lanes = [jnp.zeros((8, 128), jnp.int32)] * rounds_of
            for g in range(group * group_rows, (group + 1) * group_rows):
                shares = [jnp.zeros((8, 128), jnp.float32)] * rounds_of
                for k in range(DEG):
                    entry = edge[k, g]
                    value = weight[k, g]
                    match = (entry >> 7) == wanted
                    number = jnp.where(match, seen, -1)
                    slot = entry & 127
                    for r in range(rounds_of):
                        take = number == r
                        lanes[r] = jnp.where(take, slot, lanes[r])
                        shares[r] = jnp.where(take, value, shares[r])
                    seen = jnp.where(match, seen + 1, seen)
                for r in range(rounds_of):
                    halo_weight[place, r, g] = shares[r]
            for r in range(rounds_of):
                halo_lane[place, r, group] = lanes[r]
            most = jnp.maximum(most, seen)
        return most

    most = lax.fori_loop(0, count, build, jnp.zeros((8, 128), jnp.int32))
    flag_out[...] = jnp.where(most > rounds_of, 1.0, 0.0)
    for place in reversed(range(count)):
        pltpu.make_async_remote_copy(
            src_ref=flag_out, dst_ref=flag_in.at[inverse[place]], send_sem=sem_flag.at[0], recv_sem=sem_flag.at[1],
            device_id={"cells": partition_at(place)}, device_id_type=MESH,
        ).start()

    def wait(ref, sem):
        pltpu.make_async_copy(ref, ref, sem).wait()

    wait(have_s.at[pl.ds(0, slabs - 1)], sem_s.at[1])
    levels = slabs * 8
    modes = [full_product(l2m_ref[...], have_s[:, piece].reshape(levels, 128)) for piece in range(share)]
    table = have_s[:, share].reshape(levels, 128)
    stages = ((0, 1), (1, 2), (2, TERMS))
    for stage, (low, high) in enumerate(stages):
        for term in range(low, high):
            scale = table[:, TERMS - 1 - term : TERMS - term]
            for piece in range(share):
                mixed = full_product(m2l_ref[...], modes[piece] * scale)
                for peer in range(slabs):
                    give_g[peer, term, piece] = mixed[peer * 8 : peer * 8 + 8]
        for step in order:
            peer = (slab + step) % slabs
            pltpu.make_async_remote_copy(
                src_ref=give_g.at[peer, pl.ds(low, high - low)],
                dst_ref=have_g.at[pl.ds(low, high - low), slab],
                send_sem=sem_g.at[0, stage], recv_sem=sem_g.at[1, stage],
                device_id={"lev": peer}, device_id_type=MESH,
            ).start()
        for term in range(low, high):
            have_g[term, slab] = give_g[slab, term]

    def wait_stage(stage):
        low, high = stages[stage]
        wait(have_g.at[pl.ds(low, high - low), pl.ds(0, slabs - 1)], sem_g.at[1, stage])

    wait_stage(0)
    for tile in range(tiles):
        field[0, tile] = have_g[0, tile // share, tile % share]
        field[1, tile] = jnp.zeros((8, 128), jnp.float32)

    half = lax.broadcasted_iota(jnp.int32, (8, 128), 1) < 64
    bits = int(math.log2(tiles))

    def application(turn, carry):
        now = turn % 2
        old = 1 - now

        @pl.when(turn >= 2)
        def _():
            wait(send.at[now], sem_send.at[now])

        for place in reversed(range(count)):
            code = pack[place]
            lanes = code & 127
            found = [lane_gather(field[now, tile], lanes) for tile in range(tiles)]
            for bit in range(bits):
                odd = (code & (128 << bit)) != 0
                found = [jnp.where(odd, found[2 * i + 1], found[2 * i]) for i in range(len(found) // 2)]
            send[now, place] = found[0]
            group = [i for i, (low, high) in enumerate(groups) if low <= inverse[place] < high][0]
            pltpu.make_async_remote_copy(
                src_ref=send.at[now, place], dst_ref=halo.at[now, inverse[place]],
                send_sem=sem_send.at[now], recv_sem=sem_recv.at[now, group],
                device_id={"cells": partition_at(place)}, device_id_type=MESH,
            ).start()

        for tile in range(tiles):
            g, t = tile // 8, tile % 8
            middle = field[now, tile]
            sides = jnp.where(half, field[now, min(tile + 1, tiles - 1)], field[now, max(tile - 1, 0)])
            value = middle * block(own[g, t : t + 1, :])
            for k in range(DEG):
                lanes = block(lane_a[k, g, t : t + 1, :])
                value = value + block(weight_a[k, g, t : t + 1, :]) * lane_gather(middle, lanes)
                value = value + block(weight_b[k, g, t : t + 1, :]) * lane_gather(sides, lanes)
            total[tile] = value

        @pl.when(turn == 0)
        def _():
            wait_stage(1)

        @pl.when(turn == 1)
        def _():
            wait_stage(2)

        scale = jnp.where(turn == TERMS - 2, 0.5, 1.0)
        for index, (low, high) in enumerate(groups):
            wait(halo.at[now, pl.ds(low, high - low)], sem_recv.at[now, index])
            for t in range(8):
                for group in range(group_count):
                    rows = range(group * group_rows, (group + 1) * group_rows)
                    values = [total[8 * g + t] for g in rows]
                    for place in range(low, high):
                        arrived = halo[now, place]
                        for r in range(rounds_of):
                            lanes = block(halo_lane[place, r, group, t : t + 1, :])
                            got = lane_gather(arrived, lanes)
                            for i, g in enumerate(rows):
                                values[i] = values[i] + block(halo_weight[place, r, g, t : t + 1, :]) * got
                    for i, g in enumerate(rows):
                        tile = 8 * g + t
                        if index < len(groups) - 1:
                            total[tile] = values[i]
                        else:
                            field[old, tile] = (
                                have_g[turn + 1, tile // share, tile % share] + scale * values[i] - field[old, tile]
                            )
        return carry

    lax.fori_loop(0, TERMS - 1, application, 0)

    last = (TERMS - 1) % 2
    for tile in range(tiles):
        out_ref[:, tile * 128 : tile * 128 + 128] = field[last, tile]

    for now in range(2):
        wait(send.at[now], sem_send.at[now])
    wait(give_s.at[pl.ds(0, slabs - 1)], sem_s.at[0])
    for stage, (low, high) in enumerate(stages):
        wait(have_g.at[pl.ds(low, high - low), pl.ds(0, slabs - 1)], sem_g.at[0, stage])
    wait(flag_in, sem_flag.at[0])
    wait(flag_in, sem_flag.at[1])
    worst = flag_out[...]
    for place in range(count):
        worst = jnp.maximum(worst, flag_in[place])
    flag_ref[...] = worst


def solve(parts, slabs, group_rows, rounds_of, number, source, l2m, m2l, shift, weights, near, lists):
    columns = source.shape[1]
    tiles = columns // 128
    eighths = tiles // 8
    share = tiles // slabs
    peers = parts - 1
    f32, i32 = jnp.float32, jnp.int32
    groups = len(peers_of(parts // 2)[1])
    vmem = pl.BlockSpec(memory_space=pltpu.VMEM)
    return pl.pallas_call(
        functools.partial(kernel, parts, slabs, group_rows, rounds_of),
        name=f"solve_{number}",
        out_shape=(
            jax.ShapeDtypeStruct(source.shape, f32),
            jax.ShapeDtypeStruct((8, 128), f32),
        ),
        in_specs=[pl.BlockSpec(memory_space=pltpu.SMEM)] + [vmem] * 6,
        out_specs=(vmem, vmem),
        scratch_shapes=[
            pltpu.VMEM((DEG, eighths, 8, 128), i32),
            pltpu.VMEM((DEG, eighths, 8, 128), f32),
            pltpu.VMEM((DEG, eighths, 8, 128), i32),
            pltpu.VMEM((DEG, eighths, 8, 128), f32),
            pltpu.VMEM((DEG, eighths, 8, 128), f32),
            pltpu.VMEM((eighths, 8, 128), f32),
            pltpu.VMEM((peers, rounds_of, eighths // group_rows, 8, 128), i32),
            pltpu.VMEM((peers, rounds_of, eighths, 8, 128), f32),
            pltpu.VMEM((peers, 8, 128), i32),
            pltpu.VMEM((slabs, share + 1, 8, 128), f32),
            pltpu.VMEM((slabs, share + 1, 8, 128), f32),
            pltpu.VMEM((slabs, TERMS, share, 8, 128), f32),
            pltpu.VMEM((TERMS, slabs, share, 8, 128), f32),
            pltpu.VMEM((2, tiles, 8, 128), f32),
            pltpu.VMEM((tiles, 8, 128), f32),
            pltpu.VMEM((2, peers, 8, 128), f32),
            pltpu.VMEM((2, peers, 8, 128), f32),
            pltpu.VMEM((8, 128), f32),
            pltpu.VMEM((peers, 8, 128), f32),
            pltpu.SemaphoreType.DMA((2,)),
            pltpu.SemaphoreType.DMA((2, 3)),
            pltpu.SemaphoreType.DMA((2,)),
            pltpu.SemaphoreType.DMA((2, groups)),
            pltpu.SemaphoreType.DMA((2,)),
        ],
        compiler_params=pltpu.CompilerParams(
            collective_id=number, has_side_effects=True, vmem_limit_bytes=40 << 20
        ),
    )(shift, source, l2m, m2l, weights, near, lists)


FAST = (4, 5)
SAFE = (1, DEG)


def solution(mesh):
    parts, slabs = mesh.shape["cells"], mesh.shape["lev"]

    def local(source, l2m, m2l, shift, weights, near, lists):
        arrays = (source, l2m, m2l, shift, weights, near, lists)
        eighths = source.shape[1] // 1024
        fast = (min(FAST[0], eighths), FAST[1])
        answer, flag = solve(parts, slabs, *fast, 0, *arrays)
        return lax.cond(
            flag[0, 0] > 0.0,
            lambda arrays, answer: solve(parts, slabs, *SAFE, 1, *arrays)[0],
            lambda arrays, answer: answer,
            arrays,
            answer,
        )

    in_specs = (P("lev", "cells"), P(), P(), P("lev"), P(None, "cells"), P(None, "cells"), P("cells", None))
    return jax.shard_map(local, mesh=mesh, in_specs=in_specs, out_specs=P("lev", "cells"), check_vma=False)
```

```python
import functools
import math

import jax
import jax.numpy as jnp
from jax import lax
from jax.experimental import pallas as pl
from jax.experimental.pallas import tpu as pltpu
from jax.sharding import PartitionSpec as P

DEG = 6
HMAX = 128
SWEEPS = 2
STEPS = 4
TERMS = SWEEPS * STEPS
RADIUS = DEG / 2.0
MESH = pl.DeviceIdType.MESH
GATHER = lax.GatherDimensionNumbers(
    offset_dims=(),
    collapsed_slice_dims=(1,),
    start_index_map=(1,),
    operand_batching_dims=(0,),
    start_indices_batching_dims=(0,),
)


def lane_gather(block, lanes):
    return lax.gather(
        block, lanes[..., None], GATHER, slice_sizes=(1, 1), mode=lax.GatherScatterMode.PROMISE_IN_BOUNDS
    )


def full_product(left, right):
    return jnp.dot(left, right, precision=lax.Precision.HIGHEST, preferred_element_type=jnp.float32)


def peers_of(chips):
    places, groups = [(0, 1)], [(0, 1)]
    for far in range(1, chips // 2 + 1):
        start = len(places)
        for step in sorted({far, chips - far}):
            places += [(step, 0), (step, 1)]
        groups.append((start, len(places)))
    return places, groups


def far_first(slabs):
    side = math.isqrt(slabs)

    def hops(step):
        along, across = step // side, step % side
        rows = -(-slabs // side)
        return min(along, rows - along) + min(across, side - across)

    return sorted(range(1, slabs), key=lambda step: -hops(step))


def block(row):
    return jnp.broadcast_to(row, (8, 128))


def chebyshev_coefficients(shift):
    lane = lax.broadcasted_iota(jnp.int32, (8, 128), 1)
    up = jnp.where(lane == 0, 0.0, jnp.where(lane == 1, 1.0, 0.5))
    down = jnp.where(lane < TERMS, 0.5, 0.0)

    def operator(poly):
        scaled = up * pltpu.roll(poly, 1, 1) + down * pltpu.roll(poly, 127, 1)
        return centre * poly + RADIUS * scaled

    centre = shift + RADIUS
    sigma = centre / RADIUS
    answer = jnp.zeros((8, 128), jnp.float32)
    remain = jnp.where(lane == 0, 1.0, 0.0)
    direction = answer
    factor = 1.0 / sigma
    for sweep_index in range(SWEEPS):
        for step_index in range(STEPS):
            if sweep_index + step_index > 0:
                remain = remain - operator(direction)
            if step_index == 0:
                factor = 1.0 / sigma
                direction = remain / centre
            else:
                newer = 1.0 / (2.0 * sigma - factor)
                direction = newer * factor * direction + (2.0 * newer / RADIUS) * remain
                factor = newer
            answer = answer + direction
    return answer


def kernel(
    parts, slabs, group_rows, rounds_of, spare,
    shift_hbm, source_hbm, l2m_hbm, m2l_hbm, weight_hbm, near_hbm, list_hbm,
    out_ref, flag_ref,
    shift_ref, source_ref, l2m_ref, m2l_ref, weight_ref, near_ref, list_ref,
    edge, weight, lane_a, weight_a, weight_b, own, halo_lane, halo_weight, extra_code, extra_weight, pack,
    give_s, have_s, modes_ref, table_ref, give_g, have_g, field, total, send, halo, flag_out, flag_in,
    sem_in, sem_s, sem_g, sem_send, sem_recv, sem_flag,
):
    loads = [
        pltpu.make_async_copy(far, near, sem_in.at[index])
        for index, (far, near) in enumerate(
            (
                (shift_hbm, shift_ref), (source_hbm, source_ref), (near_hbm, near_ref), (weight_hbm, weight_ref),
                (list_hbm, list_ref), (l2m_hbm, l2m_ref), (m2l_hbm, m2l_ref),
            )
        )
    ]
    for load in loads:
        load.start()
    columns = source_ref.shape[1]
    tiles = columns // 128
    eighths = tiles // 8
    share = tiles // slabs
    part = lax.axis_index("cells")
    slab = lax.axis_index("lev")
    chips = parts // 2
    places, groups = peers_of(chips)
    count = len(places)
    chip, core = part // 2, part % 2
    inverse = [places.index(((chips - step) % chips, swap)) for step, swap in places]

    def partition_at(place):
        step, swap = places[place]
        return ((chip + step) % chips) * 2 + (core + swap) % 2

    barrier = pltpu.get_barrier_semaphore()
    order = far_first(slabs)
    order2 = sorted(range(1, slabs), key=lambda step: -(step * 7 % slabs))
    for place in reversed(range(count)):
        pl.semaphore_signal(barrier, inc=1, device_id={"cells": partition_at(place)}, device_id_type=MESH)
        turn = count - 1 - place
        if turn < slabs - 1:
            peer = (slab + order[turn]) % slabs
            pl.semaphore_signal(barrier, inc=1, device_id={"lev": peer}, device_id_type=MESH)
    for step in order[count:]:
        pl.semaphore_signal(barrier, inc=1, device_id={"lev": (slab + step) % slabs}, device_id_type=MESH)

    row = lax.broadcasted_iota(jnp.int32, (8, 128), 0)
    loads[0].wait()
    square = (8, 8)
    diagonal = lax.broadcasted_iota(jnp.int32, square, 0) == lax.broadcasted_iota(jnp.int32, square, 1)
    shift = jnp.where(diagonal, jnp.broadcast_to(shift_ref[...].reshape(1, 8), square), 0.0)
    shift = jnp.broadcast_to(jnp.sum(shift, axis=1, keepdims=True), (8, 128))
    coefficients = chebyshev_coefficients(shift)
    loads[1].wait()
    for peer in range(slabs):
        for piece in range(share):
            at = (peer * share + piece) * 128
            give_s[peer, piece] = source_ref[:, at : at + 128]
        give_s[peer, share] = coefficients
    have_s[slab] = give_s[slab]

    pl.semaphore_wait(barrier, count + slabs - 1)

    for step in order:
        peer = (slab + step) % slabs
        pltpu.make_async_remote_copy(
            src_ref=give_s.at[peer], dst_ref=have_s.at[slab], send_sem=sem_s.at[0], recv_sem=sem_s.at[1],
            device_id={"lev": peer}, device_id_type=MESH,
        ).start()

    for load in loads[2:5]:
        load.wait()
    for k in range(DEG):
        for tile in range(tiles):
            edge[k, tile // 8, tile % 8 : tile % 8 + 1, :] = near_ref[k : k + 1, tile * 128 : tile * 128 + 128]
            weight[k, tile // 8, tile % 8 : tile % 8 + 1, :] = weight_ref[k : k + 1, tile * 128 : tile * 128 + 128]
    for g in range(eighths):
        diagonal = jnp.zeros((8, 128), jnp.float32)
        for k in range(DEG):
            entry = edge[k, g]
            value = weight[k, g]
            diagonal = diagonal + value
            scaled = value * (-2.0 / RADIUS)
            inside = entry < columns
            here = (entry >> 7) == (row + 8 * g)
            lane_a[k, g] = entry & 127
            weight_a[k, g] = jnp.where(here, scaled, 0.0)
            weight_b[k, g] = jnp.where(inside, jnp.where(here, 0.0, scaled), 0.0)
            edge[k, g] = jnp.where(inside, -1, entry - columns)
            weight[k, g] = scaled
        own[g] = (diagonal - RADIUS) * (2.0 / RADIUS)
    for place in range(count):
        start = pl.multiple_of(partition_at(place) * HMAX, HMAX)
        pack[place] = block(list_ref[0:1, pl.ds(start, HMAX)])

    group_count = eighths // group_rows

    zero = jnp.zeros((8, 128), jnp.float32)
    none = jnp.zeros((8, 128), jnp.int32)

    def partition_from(place):
        pair = (place + 1) // 2
        step = jnp.where(pair % 2 == 1, (pair + 1) // 2, chips - pair // 2)
        step = jnp.where(pair == 0, 0, step)
        return ((chip + step) % chips) * 2 + (core + (place + 1) % 2) % 2

    def build(place, carry):
        most, left, codes, values = carry
        codes, values = list(codes), list(values)
        wanted = partition_from(place)
        for group in range(group_count):
            seen = none
            lanes = [none] * rounds_of
            for g in range(group * group_rows, (group + 1) * group_rows):
                shares = [zero] * rounds_of
                for k in range(DEG):
                    entry = edge[k, g]
                    value = weight[k, g]
                    match = (entry >> 7) == wanted
                    number = jnp.where(match, seen, -1)
                    slot = entry & 127
                    for r in range(rounds_of):
                        take = number == r
                        lanes[r] = jnp.where(take, slot, lanes[r])
                        shares[r] = jnp.where(take, value, shares[r])
                    seen = jnp.where(match, seen + 1, seen)
                    if spare:
                        over = number >= rounds_of
                        number = jnp.where(over, left, -1)
                        for q in range(spare):
                            take = number == q
                            codes[q] = jnp.where(take, entry + g * width, codes[q])
                            values[q] = jnp.where(take, value, values[q])
                        left = jnp.where(over, left + 1, left)
                for r in range(rounds_of):
                    halo_weight[place, r, g] = shares[r]
            for r in range(rounds_of):
                halo_lane[place, r, group] = lanes[r]
            most = jnp.maximum(most, seen)
        return most, left, tuple(codes), tuple(values)

    width = parts * HMAX
    most, left, codes, values = lax.fori_loop(
        0, count, build, (none, none, (none - 1,) * spare, (zero,) * spare)
    )
    if spare:
        before = none
        running = left
        for row_shift in (1, 2, 4):
            running = running + jnp.where(row >= row_shift, pltpu.roll(running, row_shift, 0), 0)
        before = running - left
        lane_total = block(jnp.max(running, axis=0, keepdims=True))
        bad = (left > spare) | (lane_total > spare)
        for slot in range(spare):
            chosen = none - 1
            amounts = [zero] * eighths
            for q in range(spare):
                take = (left > q) & (before + q == slot)
                chosen = jnp.where(take, codes[q] % width, chosen)
                for g in range(eighths):
                    amounts[g] = jnp.where(take & (codes[q] // width == g), values[q], amounts[g])
            extra_code[slot] = block(jnp.max(chosen, axis=0, keepdims=True))
            for g in range(eighths):
                extra_weight[slot, g] = amounts[g]
    else:
        bad = most > rounds_of
    flag_out[...] = jnp.where(bad, 1.0, 0.0)
    for place in reversed(range(count)):
        pltpu.make_async_remote_copy(
            src_ref=flag_out, dst_ref=flag_in.at[inverse[place]], send_sem=sem_flag.at[0], recv_sem=sem_flag.at[1],
            device_id={"cells": partition_at(place)}, device_id_type=MESH,
        ).start()

    def wait(ref, sem):
        pltpu.make_async_copy(ref, ref, sem).wait()

    loads[5].wait()
    loads[6].wait()
    wait(have_s.at[pl.ds(0, slabs - 1)], sem_s.at[1])
    levels = slabs * 8
    for piece in range(share):
        modes_ref[piece] = full_product(l2m_ref[...], have_s[:, piece].reshape(levels, 128))
    table_ref[...] = have_s[:, share].reshape(levels, 128)
    column = lax.broadcasted_iota(jnp.int32, (levels, 128), 1)

    def mix_and_send(term):
        scale = jnp.sum(jnp.where(column == TERMS - 1 - term, table_ref[...], 0.0), axis=1, keepdims=True)
        for piece in range(share):
            mixed = full_product(m2l_ref[...], modes_ref[piece] * scale)
            for peer in range(slabs):
                give_g[peer, term, piece] = mixed[peer * 8 : peer * 8 + 8]
        for step in order2:
            peer = (slab + step) % slabs
            pltpu.make_async_remote_copy(
                src_ref=give_g.at[peer, term], dst_ref=have_g.at[term, slab],
                send_sem=sem_g.at[0, term], recv_sem=sem_g.at[1, term],
                device_id={"lev": peer}, device_id_type=MESH,
            ).start()
        have_g[term, slab] = give_g[slab, term]

    def wait_term(term, way):
        wait(have_g.at[term, pl.ds(0, slabs - 1)], sem_g.at[way, term])

    mix_and_send(0)
    mix_and_send(1)
    wait_term(0, 1)
    for tile in range(tiles):
        field[0, tile] = have_g[0, tile // share, tile % share]
        field[1, tile] = jnp.zeros((8, 128), jnp.float32)

    half = lax.broadcasted_iota(jnp.int32, (8, 128), 1) < 64
    bits = int(math.log2(tiles))

    def application(turn, carry):
        now = turn % 2
        old = 1 - now

        @pl.when(turn >= 2)
        def _():
            wait(send.at[now], sem_send.at[now])

        for low, high in reversed(groups):
            for place in range(low, high):
                code = pack[place]
                lanes = code & 127
                found = [lane_gather(field[now, tile], lanes) for tile in range(tiles)]
                for bit in range(bits):
                    odd = (code & (128 << bit)) != 0
                    found = [jnp.where(odd, found[2 * i + 1], found[2 * i]) for i in range(len(found) // 2)]
                send[now, place] = found[0]
            for place in range(low, high):
                pltpu.make_async_remote_copy(
                    src_ref=send.at[now, place], dst_ref=halo.at[now, inverse[place]],
                    send_sem=sem_send.at[now], recv_sem=sem_recv.at[now, groups.index((low, high))],
                    device_id={"cells": partition_at(place)}, device_id_type=MESH,
                ).start()

        @pl.when(turn + 2 < TERMS)
        def _():
            mix_and_send(turn + 2)

        for tile in range(tiles):
            g, t = tile // 8, tile % 8
            middle = field[now, tile]
            sides = jnp.where(half, field[now, min(tile + 1, tiles - 1)], field[now, max(tile - 1, 0)])
            value = middle * block(own[g, t : t + 1, :])
            for k in range(DEG):
                lanes = block(lane_a[k, g, t : t + 1, :])
                value = value + block(weight_a[k, g, t : t + 1, :]) * lane_gather(middle, lanes)
                value = value + block(weight_b[k, g, t : t + 1, :]) * lane_gather(sides, lanes)
            total[tile] = value

        @pl.when(turn == 0)
        def _():
            wait(flag_in, sem_flag.at[0])
            wait(flag_in, sem_flag.at[1])
            worst = flag_out[...]
            for place in range(count):
                worst = jnp.maximum(worst, flag_in[place])
            flag_ref[0, 0] = jnp.max(worst).astype(jnp.int32)

        wait_term(turn + 1, 1)
        scale = jnp.where(turn == TERMS - 2, 0.5, 1.0)
        extras = [zero] * spare
        for index, (low, high) in enumerate(groups):
            wait(halo.at[now, pl.ds(low, high - low)], sem_recv.at[now, index])
            last_group = index == len(groups) - 1
            for place in range(low, high):
                for slot in range(spare):
                    code = extra_code[slot]
                    got = lane_gather(halo[now, place], code & 127)
                    extras[slot] = jnp.where((code >> 7) == partition_at(place), got, extras[slot])
            for t in range(8):
                for group in range(group_count):
                    rows = range(group * group_rows, (group + 1) * group_rows)
                    values = [total[8 * g + t] for g in rows]
                    for place in range(low, high):
                        arrived = halo[now, place]
                        for r in range(rounds_of):
                            lanes = block(halo_lane[place, r, group, t : t + 1, :])
                            got = lane_gather(arrived, lanes)
                            for i, g in enumerate(rows):
                                values[i] = values[i] + block(halo_weight[place, r, g, t : t + 1, :]) * got
                    for i, g in enumerate(rows):
                        tile = 8 * g + t
                        if not last_group:
                            total[tile] = values[i]
                        else:
                            for slot in range(spare):
                                values[i] = values[i] + block(extra_weight[slot, g, t : t + 1, :]) * extras[slot]
                            field[old, tile] = (
                                have_g[turn + 1, tile // share, tile % share] + scale * values[i] - field[old, tile]
                            )
        return carry

    lax.fori_loop(0, TERMS - 1, application, 0)

    last = (TERMS - 1) % 2
    for tile in range(tiles):
        out_ref[:, tile * 128 : tile * 128 + 128] = field[last, tile]

    for now in range(2):
        wait(send.at[now], sem_send.at[now])
    wait(give_s.at[pl.ds(0, slabs - 1)], sem_s.at[0])
    for term in range(TERMS):
        wait_term(term, 0)


def solve(parts, slabs, group_rows, rounds_of, spare, number, source, l2m, m2l, shift, weights, near, lists):
    columns = source.shape[1]
    tiles = columns // 128
    eighths = tiles // 8
    share = tiles // slabs
    peers = parts - 1
    f32, i32 = jnp.float32, jnp.int32
    groups = len(peers_of(parts // 2)[1])
    slots = max(spare, 1)
    return pl.pallas_call(
        functools.partial(kernel, parts, slabs, group_rows, rounds_of, spare),
        name=f"solve_{number}",
        out_shape=(
            jax.ShapeDtypeStruct(source.shape, f32),
            jax.ShapeDtypeStruct((1, 1), i32),
        ),
        in_specs=[pl.BlockSpec(memory_space=pltpu.HBM)] * 7,
        out_specs=(pl.BlockSpec(memory_space=pltpu.VMEM), pl.BlockSpec(memory_space=pltpu.SMEM)),
        scratch_shapes=[
            pltpu.VMEM(shift.shape, f32),
            pltpu.VMEM(source.shape, f32),
            pltpu.VMEM(l2m.shape, f32),
            pltpu.VMEM(m2l.shape, f32),
            pltpu.VMEM(weights.shape, f32),
            pltpu.VMEM(near.shape, i32),
            pltpu.VMEM(lists.shape, i32),
            pltpu.VMEM((DEG, eighths, 8, 128), i32),
            pltpu.VMEM((DEG, eighths, 8, 128), f32),
            pltpu.VMEM((DEG, eighths, 8, 128), i32),
            pltpu.VMEM((DEG, eighths, 8, 128), f32),
            pltpu.VMEM((DEG, eighths, 8, 128), f32),
            pltpu.VMEM((eighths, 8, 128), f32),
            pltpu.VMEM((peers, rounds_of, eighths // group_rows, 8, 128), i32),
            pltpu.VMEM((peers, rounds_of, eighths, 8, 128), f32),
            pltpu.VMEM((slots, 8, 128), i32),
            pltpu.VMEM((slots, eighths, 8, 128), f32),
            pltpu.VMEM((peers, 8, 128), i32),
            pltpu.VMEM((slabs, share + 1, 8, 128), f32),
            pltpu.VMEM((slabs, share + 1, 8, 128), f32),
            pltpu.VMEM((share, l2m.shape[0], 128), f32),
            pltpu.VMEM((l2m.shape[0], 128), f32),
            pltpu.VMEM((slabs, TERMS, share, 8, 128), f32),
            pltpu.VMEM((TERMS, slabs, share, 8, 128), f32),
            pltpu.VMEM((2, tiles, 8, 128), f32),
            pltpu.VMEM((tiles, 8, 128), f32),
            pltpu.VMEM((2, peers, 8, 128), f32),
            pltpu.VMEM((2, peers, 8, 128), f32),
            pltpu.VMEM((8, 128), f32),
            pltpu.VMEM((peers, 8, 128), f32),
            pltpu.SemaphoreType.DMA((7,)),
            pltpu.SemaphoreType.DMA((2,)),
            pltpu.SemaphoreType.DMA((2, TERMS)),
            pltpu.SemaphoreType.DMA((2,)),
            pltpu.SemaphoreType.DMA((2, groups)),
            pltpu.SemaphoreType.DMA((2,)),
        ],
        compiler_params=pltpu.CompilerParams(
            collective_id=number, has_side_effects=True, vmem_limit_bytes=40 << 20
        ),
    )(shift, source, l2m, m2l, weights, near, lists)


FAST = (4, 2, 3)
SAFE = (1, DEG, 0)


def solution(mesh):
    parts, slabs = mesh.shape["cells"], mesh.shape["lev"]

    def local(source, l2m, m2l, shift, weights, near, lists):
        arrays = (source, l2m, m2l, shift, weights, near, lists)
        eighths = source.shape[1] // 1024
        fast = (min(FAST[0], eighths), *FAST[1:])
        answer, flag = solve(parts, slabs, *fast, 0, *arrays)
        return lax.switch(
            flag[0, 0],
            (
                lambda arrays, answer: answer,
                lambda arrays, answer: solve(parts, slabs, *SAFE, 1, *arrays)[0],
            ),
            arrays,
            answer,
        )

    in_specs = (P("lev", "cells"), P(), P(), P("lev"), P(None, "cells"), P(None, "cells"), P("cells", None))
    return jax.shard_map(local, mesh=mesh, in_specs=in_specs, out_specs=P("lev", "cells"), check_vma=False)
```

```python
import functools
import math

import jax
import jax.numpy as jnp
from jax import lax
from jax.experimental import pallas as pl
from jax.experimental.pallas import tpu as pltpu
from jax.sharding import PartitionSpec as P

DEG = 6
HMAX = 128
SWEEPS = 2
STEPS = 4
TERMS = SWEEPS * STEPS
RADIUS = DEG / 2.0
MESH = pl.DeviceIdType.MESH
GATHER = lax.GatherDimensionNumbers(
    offset_dims=(),
    collapsed_slice_dims=(1,),
    start_index_map=(1,),
    operand_batching_dims=(0,),
    start_indices_batching_dims=(0,),
)


def lane_gather(block, lanes):
    return lax.gather(
        block, lanes[..., None], GATHER, slice_sizes=(1, 1), mode=lax.GatherScatterMode.PROMISE_IN_BOUNDS
    )


def full_product(left, right):
    return jnp.dot(left, right, precision=lax.Precision.HIGHEST, preferred_element_type=jnp.float32)


def peers_of(chips):
    places, groups = [(0, 1)], [(0, 1)]
    for far in range(1, chips // 2 + 1):
        start = len(places)
        for step in sorted({far, chips - far}):
            places += [(step, 0), (step, 1)]
        groups.append((start, len(places)))
    return places, groups


def far_first(slabs):
    side = math.isqrt(slabs)

    def hops(step):
        along, across = step // side, step % side
        rows = -(-slabs // side)
        return min(along, rows - along) + min(across, side - across)

    return sorted(range(1, slabs), key=lambda step: -hops(step))


def block(row):
    return jnp.broadcast_to(row, (8, 128))


def chebyshev_coefficients(shift):
    lane = lax.broadcasted_iota(jnp.int32, (8, 128), 1)
    up = jnp.where(lane == 0, 0.0, jnp.where(lane == 1, 1.0, 0.5))
    down = jnp.where(lane < TERMS, 0.5, 0.0)

    def operator(poly):
        scaled = up * pltpu.roll(poly, 1, 1) + down * pltpu.roll(poly, 127, 1)
        return centre * poly + RADIUS * scaled

    centre = shift + RADIUS
    sigma = centre / RADIUS
    answer = jnp.zeros((8, 128), jnp.float32)
    remain = jnp.where(lane == 0, 1.0, 0.0)
    direction = answer
    factor = 1.0 / sigma
    for sweep_index in range(SWEEPS):
        for step_index in range(STEPS):
            if sweep_index + step_index > 0:
                remain = remain - operator(direction)
            if step_index == 0:
                factor = 1.0 / sigma
                direction = remain / centre
            else:
                newer = 1.0 / (2.0 * sigma - factor)
                direction = newer * factor * direction + (2.0 * newer / RADIUS) * remain
                factor = newer
            answer = answer + direction
    return answer


def kernel(
    parts, slabs, group_rows, rounds_of, spare,
    shift_hbm, source_hbm, l2m_hbm, m2l_hbm, weight_hbm, near_hbm, list_hbm,
    out_ref, flag_ref,
    shift_ref, source_ref, l2m_ref, m2l_ref, weight_ref, near_ref, list_ref,
    edge, weight, lane_a, weight_a, weight_b, own, halo_lane, halo_weight, extra_code, extra_weight, pack,
    give_s, have_s, modes_ref, table_ref, give_g, have_g, field, total, send, halo, flag_out, flag_in,
    sem_in, sem_s, sem_g, sem_send, sem_recv, sem_flag,
):
    loads = [
        pltpu.make_async_copy(far, near, sem_in.at[index])
        for index, (far, near) in enumerate(
            (
                (shift_hbm, shift_ref), (source_hbm, source_ref), (near_hbm, near_ref), (weight_hbm, weight_ref),
                (list_hbm, list_ref), (l2m_hbm, l2m_ref), (m2l_hbm, m2l_ref),
            )
        )
    ]
    for load in loads:
        load.start()
    columns = source_ref.shape[1]
    tiles = columns // 128
    eighths = tiles // 8
    share = tiles // slabs
    part = lax.axis_index("cells")
    slab = lax.axis_index("lev")
    chips = parts // 2
    places, groups = peers_of(chips)
    count = len(places)
    chip, core = part // 2, part % 2
    inverse = [places.index(((chips - step) % chips, swap)) for step, swap in places]

    def partition_at(place):
        step, swap = places[place]
        return ((chip + step) % chips) * 2 + (core + swap) % 2

    barrier = pltpu.get_barrier_semaphore()
    order = far_first(slabs)
    order2 = sorted(range(1, slabs), key=lambda step: -(step * 7 % slabs))
    for place in reversed(range(count)):
        pl.semaphore_signal(barrier, inc=1, device_id={"cells": partition_at(place)}, device_id_type=MESH)
        turn = count - 1 - place
        if turn < slabs - 1:
            peer = (slab + order[turn]) % slabs
            pl.semaphore_signal(barrier, inc=1, device_id={"lev": peer}, device_id_type=MESH)
    for step in order[count:]:
        pl.semaphore_signal(barrier, inc=1, device_id={"lev": (slab + step) % slabs}, device_id_type=MESH)

    row = lax.broadcasted_iota(jnp.int32, (8, 128), 0)
    loads[0].wait()
    square = (8, 8)
    diagonal = lax.broadcasted_iota(jnp.int32, square, 0) == lax.broadcasted_iota(jnp.int32, square, 1)
    shift = jnp.where(diagonal, jnp.broadcast_to(shift_ref[...].reshape(1, 8), square), 0.0)
    shift = jnp.broadcast_to(jnp.sum(shift, axis=1, keepdims=True), (8, 128))
    coefficients = chebyshev_coefficients(shift)
    loads[1].wait()
    for peer in range(slabs):
        for piece in range(share):
            at = (peer * share + piece) * 128
            give_s[peer, piece] = source_ref[:, at : at + 128]
        give_s[peer, share] = coefficients
    have_s[slab] = give_s[slab]

    pl.semaphore_wait(barrier, count + slabs - 1)

    for step in order:
        peer = (slab + step) % slabs
        pltpu.make_async_remote_copy(
            src_ref=give_s.at[peer], dst_ref=have_s.at[slab], send_sem=sem_s.at[0], recv_sem=sem_s.at[1],
            device_id={"lev": peer}, device_id_type=MESH,
        ).start()

    for load in loads[2:5]:
        load.wait()
    for k in range(DEG):
        for tile in range(tiles):
            edge[k, tile // 8, tile % 8 : tile % 8 + 1, :] = near_ref[k : k + 1, tile * 128 : tile * 128 + 128]
            weight[k, tile // 8, tile % 8 : tile % 8 + 1, :] = weight_ref[k : k + 1, tile * 128 : tile * 128 + 128]
    for g in range(eighths):
        diagonal = jnp.zeros((8, 128), jnp.float32)
        for k in range(DEG):
            entry = edge[k, g]
            value = weight[k, g]
            diagonal = diagonal + value
            scaled = value * (-2.0 / RADIUS)
            inside = entry < columns
            here = (entry >> 7) == (row + 8 * g)
            lane_a[k, g] = entry & 127
            weight_a[k, g] = jnp.where(here, scaled, 0.0)
            weight_b[k, g] = jnp.where(inside, jnp.where(here, 0.0, scaled), 0.0)
            edge[k, g] = jnp.where(inside, -1, entry - columns)
            weight[k, g] = scaled
        own[g] = (diagonal - RADIUS) * (2.0 / RADIUS)
    for place in range(count):
        start = pl.multiple_of(partition_at(place) * HMAX, HMAX)
        pack[place] = block(list_ref[0:1, pl.ds(start, HMAX)])

    group_count = eighths // group_rows

    zero = jnp.zeros((8, 128), jnp.float32)
    none = jnp.zeros((8, 128), jnp.int32)

    def partition_from(place):
        pair = (place + 1) // 2
        step = jnp.where(pair % 2 == 1, (pair + 1) // 2, chips - pair // 2)
        step = jnp.where(pair == 0, 0, step)
        return ((chip + step) % chips) * 2 + (core + (place + 1) % 2) % 2

    def build(place, carry):
        most, left, codes, values = carry
        codes, values = list(codes), list(values)
        wanted = partition_from(place)
        for group in range(group_count):
            seen = none
            lanes = [none] * rounds_of
            for g in range(group * group_rows, (group + 1) * group_rows):
                shares = [zero] * rounds_of
                for k in range(DEG):
                    entry = edge[k, g]
                    value = weight[k, g]
                    match = (entry >> 7) == wanted
                    number = jnp.where(match, seen, -1)
                    slot = entry & 127
                    for r in range(rounds_of):
                        take = number == r
                        lanes[r] = jnp.where(take, slot, lanes[r])
                        shares[r] = jnp.where(take, value, shares[r])
                    seen = jnp.where(match, seen + 1, seen)
                    if spare:
                        over = number >= rounds_of
                        number = jnp.where(over, left, -1)
                        for q in range(spare):
                            take = number == q
                            codes[q] = jnp.where(take, entry + g * width, codes[q])
                            values[q] = jnp.where(take, value, values[q])
                        left = jnp.where(over, left + 1, left)
                for r in range(rounds_of):
                    halo_weight[place, r, g] = shares[r]
            for r in range(rounds_of):
                halo_lane[place, r, group] = lanes[r]
            most = jnp.maximum(most, seen)
        return most, left, tuple(codes), tuple(values)

    width = parts * HMAX
    most, left, codes, values = lax.fori_loop(
        0, count, build, (none, none, (none - 1,) * spare, (zero,) * spare)
    )
    if spare:
        before = none
        running = left
        for row_shift in (1, 2, 4):
            running = running + jnp.where(row >= row_shift, pltpu.roll(running, row_shift, 0), 0)
        before = running - left
        lane_total = block(jnp.max(running, axis=0, keepdims=True))
        bad = (left > spare) | (lane_total > spare)
        for slot in range(spare):
            chosen = none - 1
            amounts = [zero] * eighths
            for q in range(spare):
                take = (left > q) & (before + q == slot)
                chosen = jnp.where(take, codes[q] % width, chosen)
                for g in range(eighths):
                    amounts[g] = jnp.where(take & (codes[q] // width == g), values[q], amounts[g])
            extra_code[slot] = block(jnp.max(chosen, axis=0, keepdims=True))
            for g in range(eighths):
                extra_weight[slot, g] = amounts[g]
    else:
        bad = most > rounds_of
    flag_out[...] = jnp.where(bad, 1.0, 0.0)
    for place in reversed(range(count)):
        pltpu.make_async_remote_copy(
            src_ref=flag_out, dst_ref=flag_in.at[inverse[place]], send_sem=sem_flag.at[0], recv_sem=sem_flag.at[1],
            device_id={"cells": partition_at(place)}, device_id_type=MESH,
        ).start()

    def wait(ref, sem):
        pltpu.make_async_copy(ref, ref, sem).wait()

    loads[5].wait()
    loads[6].wait()
    wait(have_s.at[pl.ds(0, slabs - 1)], sem_s.at[1])
    levels = slabs * 8
    for piece in range(share):
        modes_ref[piece] = full_product(l2m_ref[...], have_s[:, piece].reshape(levels, 128))
    table_ref[...] = have_s[:, share].reshape(levels, 128)
    column = lax.broadcasted_iota(jnp.int32, (levels, 128), 1)

    def mix_and_send(term):
        scale = jnp.sum(jnp.where(column == TERMS - 1 - term, table_ref[...], 0.0), axis=1, keepdims=True)
        for piece in range(share):
            mixed = full_product(m2l_ref[...], modes_ref[piece] * scale)
            for peer in range(slabs):
                give_g[peer, term, piece] = mixed[peer * 8 : peer * 8 + 8]
        for step in order2:
            peer = (slab + step) % slabs
            pltpu.make_async_remote_copy(
                src_ref=give_g.at[peer, term], dst_ref=have_g.at[term, slab],
                send_sem=sem_g.at[0, term], recv_sem=sem_g.at[1, term],
                device_id={"lev": peer}, device_id_type=MESH,
            ).start()
        have_g[term, slab] = give_g[slab, term]

    def wait_term(term, way):
        wait(have_g.at[term, pl.ds(0, slabs - 1)], sem_g.at[way, term])

    mix_and_send(0)
    mix_and_send(1)
    wait_term(0, 1)
    for tile in range(tiles):
        field[0, tile] = have_g[0, tile // share, tile % share]
        field[1, tile] = jnp.zeros((8, 128), jnp.float32)

    half = lax.broadcasted_iota(jnp.int32, (8, 128), 1) < 64
    bits = int(math.log2(tiles))

    def application(turn, carry):
        now = turn % 2
        old = 1 - now

        @pl.when(turn >= 2)
        def _():
            wait(send.at[now], sem_send.at[now])

        whole = [field[now, tile] for tile in range(tiles)]
        codes = [pack[place] for place in range(count)]
        for low, high in reversed(groups):
            for place in range(low, high):
                code = codes[place]
                lanes = code & 127
                found = [lane_gather(whole[tile], lanes) for tile in range(tiles)]
                for bit in range(bits):
                    odd = (code & (128 << bit)) != 0
                    found = [jnp.where(odd, found[2 * i + 1], found[2 * i]) for i in range(len(found) // 2)]
                send[now, place] = found[0]
            for place in range(low, high):
                pltpu.make_async_remote_copy(
                    src_ref=send.at[now, place], dst_ref=halo.at[now, inverse[place]],
                    send_sem=sem_send.at[now], recv_sem=sem_recv.at[now, groups.index((low, high))],
                    device_id={"cells": partition_at(place)}, device_id_type=MESH,
                ).start()

        @pl.when(turn + 2 < TERMS)
        def _():
            mix_and_send(turn + 2)

        for tile in range(tiles):
            g, t = tile // 8, tile % 8
            middle = field[now, tile]
            sides = jnp.where(half, field[now, min(tile + 1, tiles - 1)], field[now, max(tile - 1, 0)])
            value = middle * block(own[g, t : t + 1, :])
            for k in range(DEG):
                lanes = block(lane_a[k, g, t : t + 1, :])
                value = value + block(weight_a[k, g, t : t + 1, :]) * lane_gather(middle, lanes)
                value = value + block(weight_b[k, g, t : t + 1, :]) * lane_gather(sides, lanes)
            total[tile] = value

        @pl.when(turn == 0)
        def _():
            wait(flag_in, sem_flag.at[0])
            wait(flag_in, sem_flag.at[1])
            worst = flag_out[...]
            for place in range(count):
                worst = jnp.maximum(worst, flag_in[place])
            flag_ref[0, 0] = jnp.max(worst).astype(jnp.int32)

        wait_term(turn + 1, 1)
        scale = jnp.where(turn == TERMS - 2, 0.5, 1.0)
        extras = [zero] * spare
        for index, (low, high) in enumerate(groups):
            wait(halo.at[now, pl.ds(low, high - low)], sem_recv.at[now, index])
            last_group = index == len(groups) - 1
            for place in range(low, high):
                for slot in range(spare):
                    code = extra_code[slot]
                    got = lane_gather(halo[now, place], code & 127)
                    extras[slot] = jnp.where((code >> 7) == partition_at(place), got, extras[slot])
            for t in range(8):
                for group in range(group_count):
                    rows = range(group * group_rows, (group + 1) * group_rows)
                    values = [total[8 * g + t] for g in rows]
                    for place in range(low, high):
                        arrived = halo[now, place]
                        for r in range(rounds_of):
                            lanes = block(halo_lane[place, r, group, t : t + 1, :])
                            got = lane_gather(arrived, lanes)
                            for i, g in enumerate(rows):
                                values[i] = values[i] + block(halo_weight[place, r, g, t : t + 1, :]) * got
                    for i, g in enumerate(rows):
                        tile = 8 * g + t
                        if not last_group:
                            total[tile] = values[i]
                        else:
                            for slot in range(spare):
                                values[i] = values[i] + block(extra_weight[slot, g, t : t + 1, :]) * extras[slot]
                            field[old, tile] = (
                                have_g[turn + 1, tile // share, tile % share] + scale * values[i] - field[old, tile]
                            )
        return carry

    lax.fori_loop(0, TERMS - 1, application, 0)

    last = (TERMS - 1) % 2
    for tile in range(tiles):
        out_ref[:, tile * 128 : tile * 128 + 128] = field[last, tile]

    for now in range(2):
        wait(send.at[now], sem_send.at[now])
    wait(give_s.at[pl.ds(0, slabs - 1)], sem_s.at[0])
    for term in range(TERMS):
        wait_term(term, 0)


def solve(parts, slabs, group_rows, rounds_of, spare, number, source, l2m, m2l, shift, weights, near, lists):
    columns = source.shape[1]
    tiles = columns // 128
    eighths = tiles // 8
    share = tiles // slabs
    peers = parts - 1
    f32, i32 = jnp.float32, jnp.int32
    groups = len(peers_of(parts // 2)[1])
    slots = max(spare, 1)
    return pl.pallas_call(
        functools.partial(kernel, parts, slabs, group_rows, rounds_of, spare),
        name=f"solve_{number}",
        out_shape=(
            jax.ShapeDtypeStruct(source.shape, f32),
            jax.ShapeDtypeStruct((1, 1), i32),
        ),
        in_specs=[pl.BlockSpec(memory_space=pltpu.HBM)] * 7,
        out_specs=(pl.BlockSpec(memory_space=pltpu.VMEM), pl.BlockSpec(memory_space=pltpu.SMEM)),
        scratch_shapes=[
            pltpu.VMEM(shift.shape, f32),
            pltpu.VMEM(source.shape, f32),
            pltpu.VMEM(l2m.shape, f32),
            pltpu.VMEM(m2l.shape, f32),
            pltpu.VMEM(weights.shape, f32),
            pltpu.VMEM(near.shape, i32),
            pltpu.VMEM(lists.shape, i32),
            pltpu.VMEM((DEG, eighths, 8, 128), i32),
            pltpu.VMEM((DEG, eighths, 8, 128), f32),
            pltpu.VMEM((DEG, eighths, 8, 128), i32),
            pltpu.VMEM((DEG, eighths, 8, 128), f32),
            pltpu.VMEM((DEG, eighths, 8, 128), f32),
            pltpu.VMEM((eighths, 8, 128), f32),
            pltpu.VMEM((peers, rounds_of, eighths // group_rows, 8, 128), i32),
            pltpu.VMEM((peers, rounds_of, eighths, 8, 128), f32),
            pltpu.VMEM((slots, 8, 128), i32),
            pltpu.VMEM((slots, eighths, 8, 128), f32),
            pltpu.VMEM((peers, 8, 128), i32),
            pltpu.VMEM((slabs, share + 1, 8, 128), f32),
            pltpu.VMEM((slabs, share + 1, 8, 128), f32),
            pltpu.VMEM((share, l2m.shape[0], 128), f32),
            pltpu.VMEM((l2m.shape[0], 128), f32),
            pltpu.VMEM((slabs, TERMS, share, 8, 128), f32),
            pltpu.VMEM((TERMS, slabs, share, 8, 128), f32),
            pltpu.VMEM((2, tiles, 8, 128), f32),
            pltpu.VMEM((tiles, 8, 128), f32),
            pltpu.VMEM((2, peers, 8, 128), f32),
            pltpu.VMEM((2, peers, 8, 128), f32),
            pltpu.VMEM((8, 128), f32),
            pltpu.VMEM((peers, 8, 128), f32),
            pltpu.SemaphoreType.DMA((7,)),
            pltpu.SemaphoreType.DMA((2,)),
            pltpu.SemaphoreType.DMA((2, TERMS)),
            pltpu.SemaphoreType.DMA((2,)),
            pltpu.SemaphoreType.DMA((2, groups)),
            pltpu.SemaphoreType.DMA((2,)),
        ],
        compiler_params=pltpu.CompilerParams(
            collective_id=number, has_side_effects=True, vmem_limit_bytes=40 << 20
        ),
    )(shift, source, l2m, m2l, weights, near, lists)


FAST = (4, 2, 3)
SAFE = (1, DEG, 0)


def solution(mesh):
    parts, slabs = mesh.shape["cells"], mesh.shape["lev"]

    def local(source, l2m, m2l, shift, weights, near, lists):
        arrays = (source, l2m, m2l, shift, weights, near, lists)
        eighths = source.shape[1] // 1024
        fast = (min(FAST[0], eighths), *FAST[1:])
        answer, flag = solve(parts, slabs, *fast, 0, *arrays)
        return lax.switch(
            flag[0, 0],
            (
                lambda arrays, answer: answer,
                lambda arrays, answer: solve(parts, slabs, *SAFE, 1, *arrays)[0],
            ),
            arrays,
            answer,
        )

    in_specs = (P("lev", "cells"), P(), P(), P("lev"), P(None, "cells"), P(None, "cells"), P("cells", None))
    return jax.shard_map(local, mesh=mesh, in_specs=in_specs, out_specs=P("lev", "cells"), check_vma=False)
```

```python
import functools
import math

import jax
import jax.numpy as jnp
from jax import lax
from jax.experimental import pallas as pl
from jax.experimental.pallas import tpu as pltpu
from jax.sharding import PartitionSpec as P

DEG = 6
HMAX = 128
SWEEPS = 2
STEPS = 4
TERMS = SWEEPS * STEPS
RADIUS = DEG / 2.0
MESH = pl.DeviceIdType.MESH
GATHER = lax.GatherDimensionNumbers(
    offset_dims=(),
    collapsed_slice_dims=(1,),
    start_index_map=(1,),
    operand_batching_dims=(0,),
    start_indices_batching_dims=(0,),
)


def lane_gather(block, lanes):
    return lax.gather(
        block, lanes[..., None], GATHER, slice_sizes=(1, 1), mode=lax.GatherScatterMode.PROMISE_IN_BOUNDS
    )


def full_product(left, right):
    return jnp.dot(left, right, precision=lax.Precision.HIGHEST, preferred_element_type=jnp.float32)


def peers_of(chips):
    places, groups = [(0, 1)], [(0, 1)]
    for far in range(1, chips // 2 + 1):
        start = len(places)
        for step in sorted({far, chips - far}):
            places += [(step, 0), (step, 1)]
        groups.append((start, len(places)))
    return places, groups


def far_first(slabs):
    side = math.isqrt(slabs)

    def hops(step):
        along, across = step // side, step % side
        rows = -(-slabs // side)
        return min(along, rows - along) + min(across, side - across)

    return sorted(range(1, slabs), key=lambda step: -hops(step))


def block(row):
    return jnp.broadcast_to(row, (8, 128))


def chebyshev_coefficients(shift):
    lane = lax.broadcasted_iota(jnp.int32, (8, 128), 1)
    up = jnp.where(lane == 0, 0.0, jnp.where(lane == 1, 1.0, 0.5))
    down = jnp.where(lane < TERMS, 0.5, 0.0)

    def operator(poly):
        scaled = up * pltpu.roll(poly, 1, 1) + down * pltpu.roll(poly, 127, 1)
        return centre * poly + RADIUS * scaled

    centre = shift + RADIUS
    sigma = centre / RADIUS
    answer = jnp.zeros((8, 128), jnp.float32)
    remain = jnp.where(lane == 0, 1.0, 0.0)
    direction = answer
    factor = 1.0 / sigma
    for sweep_index in range(SWEEPS):
        for step_index in range(STEPS):
            if sweep_index + step_index > 0:
                remain = remain - operator(direction)
            if step_index == 0:
                factor = 1.0 / sigma
                direction = remain / centre
            else:
                newer = 1.0 / (2.0 * sigma - factor)
                direction = newer * factor * direction + (2.0 * newer / RADIUS) * remain
                factor = newer
            answer = answer + direction
    return answer


def kernel(
    parts, slabs, group_rows, rounds_of, spare,
    shift_hbm, source_hbm, l2m_hbm, m2l_hbm, weight_hbm, near_hbm, list_hbm,
    out_ref, flag_ref,
    shift_ref, source_ref, l2m_ref, m2l_ref, weight_ref, near_ref, list_ref,
    edge, weight, lane_a, weight_a, weight_b, own, halo_lane, halo_weight, extra_code, extra_weight, pack,
    give_s, have_s, modes_ref, table_ref, give_g, have_g, field, total, send, halo, flag_out, flag_in,
    sem_in, sem_s, sem_g, sem_send, sem_recv, sem_flag,
):
    loads = [
        pltpu.make_async_copy(far, near, sem_in.at[index])
        for index, (far, near) in enumerate(
            (
                (shift_hbm, shift_ref), (source_hbm, source_ref), (near_hbm, near_ref), (weight_hbm, weight_ref),
                (list_hbm, list_ref), (l2m_hbm, l2m_ref), (m2l_hbm, m2l_ref),
            )
        )
    ]
    for load in loads:
        load.start()
    columns = source_ref.shape[1]
    tiles = columns // 128
    eighths = tiles // 8
    share = tiles // slabs
    part = lax.axis_index("cells")
    slab = lax.axis_index("lev")
    chips = parts // 2
    places, groups = peers_of(chips)
    count = len(places)
    chip, core = part // 2, part % 2
    inverse = [places.index(((chips - step) % chips, swap)) for step, swap in places]

    def partition_at(place):
        step, swap = places[place]
        return ((chip + step) % chips) * 2 + (core + swap) % 2

    barrier = pltpu.get_barrier_semaphore()
    order = far_first(slabs)
    order2 = sorted(range(1, slabs), key=lambda step: -(step * 7 % slabs))
    for place in reversed(range(count)):
        pl.semaphore_signal(barrier, inc=1, device_id={"cells": partition_at(place)}, device_id_type=MESH)
        turn = count - 1 - place
        if turn < slabs - 1:
            peer = (slab + order[turn]) % slabs
            pl.semaphore_signal(barrier, inc=1, device_id={"lev": peer}, device_id_type=MESH)
    for step in order[count:]:
        pl.semaphore_signal(barrier, inc=1, device_id={"lev": (slab + step) % slabs}, device_id_type=MESH)

    row = lax.broadcasted_iota(jnp.int32, (8, 128), 0)
    loads[0].wait()
    square = (8, 8)
    diagonal = lax.broadcasted_iota(jnp.int32, square, 0) == lax.broadcasted_iota(jnp.int32, square, 1)
    shift = jnp.where(diagonal, jnp.broadcast_to(shift_ref[...].reshape(1, 8), square), 0.0)
    shift = jnp.broadcast_to(jnp.sum(shift, axis=1, keepdims=True), (8, 128))
    coefficients = chebyshev_coefficients(shift)
    loads[1].wait()
    for peer in range(slabs):
        for piece in range(share):
            at = (peer * share + piece) * 128
            give_s[peer, piece] = source_ref[:, at : at + 128]
        give_s[peer, share] = coefficients
    have_s[slab] = give_s[slab]

    pl.semaphore_wait(barrier, count + slabs - 1)

    for step in order:
        peer = (slab + step) % slabs
        pltpu.make_async_remote_copy(
            src_ref=give_s.at[peer, pl.ds(0, share)], dst_ref=have_s.at[slab, pl.ds(0, share)],
            send_sem=sem_s.at[0], recv_sem=sem_s.at[1],
            device_id={"lev": peer}, device_id_type=MESH,
        ).start()
    for step in order:
        peer = (slab + step) % slabs
        pltpu.make_async_remote_copy(
            src_ref=give_s.at[peer, share], dst_ref=have_s.at[slab, share],
            send_sem=sem_s.at[2], recv_sem=sem_s.at[3],
            device_id={"lev": peer}, device_id_type=MESH,
        ).start()

    for load in loads[2:5]:
        load.wait()
    for k in range(DEG):
        for tile in range(tiles):
            edge[k, tile // 8, tile % 8 : tile % 8 + 1, :] = near_ref[k : k + 1, tile * 128 : tile * 128 + 128]
            weight[k, tile // 8, tile % 8 : tile % 8 + 1, :] = weight_ref[k : k + 1, tile * 128 : tile * 128 + 128]
    for g in range(eighths):
        diagonal = jnp.zeros((8, 128), jnp.float32)
        for k in range(DEG):
            entry = edge[k, g]
            value = weight[k, g]
            diagonal = diagonal + value
            scaled = value * (-2.0 / RADIUS)
            inside = entry < columns
            here = (entry >> 7) == (row + 8 * g)
            lane_a[k, g] = entry & 127
            weight_a[k, g] = jnp.where(here, scaled, 0.0)
            weight_b[k, g] = jnp.where(inside, jnp.where(here, 0.0, scaled), 0.0)
            edge[k, g] = jnp.where(inside, -1, entry - columns)
            weight[k, g] = scaled
        own[g] = (diagonal - RADIUS) * (2.0 / RADIUS)
    for place in range(count):
        start = pl.multiple_of(partition_at(place) * HMAX, HMAX)
        pack[place] = block(list_ref[0:1, pl.ds(start, HMAX)])

    group_count = eighths // group_rows

    zero = jnp.zeros((8, 128), jnp.float32)
    none = jnp.zeros((8, 128), jnp.int32)

    def partition_from(place):
        pair = (place + 1) // 2
        step = jnp.where(pair % 2 == 1, (pair + 1) // 2, chips - pair // 2)
        step = jnp.where(pair == 0, 0, step)
        return ((chip + step) % chips) * 2 + (core + (place + 1) % 2) % 2

    def build(place, carry):
        most, left, codes, values = carry
        codes, values = list(codes), list(values)
        wanted = partition_from(place)
        for group in range(group_count):
            seen = none
            lanes = [none] * rounds_of
            for g in range(group * group_rows, (group + 1) * group_rows):
                shares = [zero] * rounds_of
                for k in range(DEG):
                    entry = edge[k, g]
                    value = weight[k, g]
                    match = (entry >> 7) == wanted
                    number = jnp.where(match, seen, -1)
                    slot = entry & 127
                    for r in range(rounds_of):
                        take = number == r
                        lanes[r] = jnp.where(take, slot, lanes[r])
                        shares[r] = jnp.where(take, value, shares[r])
                    seen = jnp.where(match, seen + 1, seen)
                    if spare:
                        over = number >= rounds_of
                        number = jnp.where(over, left, -1)
                        for q in range(spare):
                            take = number == q
                            codes[q] = jnp.where(take, entry + g * width, codes[q])
                            values[q] = jnp.where(take, value, values[q])
                        left = jnp.where(over, left + 1, left)
                for r in range(rounds_of):
                    halo_weight[place, r, g] = shares[r]
            for r in range(rounds_of):
                halo_lane[place, r, group] = lanes[r]
            most = jnp.maximum(most, seen)
        return most, left, tuple(codes), tuple(values)

    width = parts * HMAX
    most, left, codes, values = lax.fori_loop(
        0, count, build, (none, none, (none - 1,) * spare, (zero,) * spare)
    )
    if spare:
        before = none
        running = left
        for row_shift in (1, 2, 4):
            running = running + jnp.where(row >= row_shift, pltpu.roll(running, row_shift, 0), 0)
        before = running - left
        lane_total = block(jnp.max(running, axis=0, keepdims=True))
        bad = (left > spare) | (lane_total > spare)
        for slot in range(spare):
            chosen = none - 1
            amounts = [zero] * eighths
            for q in range(spare):
                take = (left > q) & (before + q == slot)
                chosen = jnp.where(take, codes[q] % width, chosen)
                for g in range(eighths):
                    amounts[g] = jnp.where(take & (codes[q] // width == g), values[q], amounts[g])
            extra_code[slot] = block(jnp.max(chosen, axis=0, keepdims=True))
            for g in range(eighths):
                extra_weight[slot, g] = amounts[g]
    else:
        bad = most > rounds_of
    flag_out[...] = jnp.where(bad, 1.0, 0.0)
    for place in reversed(range(count)):
        pltpu.make_async_remote_copy(
            src_ref=flag_out, dst_ref=flag_in.at[inverse[place]], send_sem=sem_flag.at[0], recv_sem=sem_flag.at[1],
            device_id={"cells": partition_at(place)}, device_id_type=MESH,
        ).start()

    def wait(ref, sem):
        pltpu.make_async_copy(ref, ref, sem).wait()

    loads[5].wait()
    loads[6].wait()
    wait(have_s.at[pl.ds(0, slabs - 1), pl.ds(0, share)], sem_s.at[1])
    levels = slabs * 8
    for piece in range(share):
        modes_ref[piece] = full_product(l2m_ref[...], have_s[:, piece].reshape(levels, 128))
    wait(have_s.at[pl.ds(0, slabs - 1), share], sem_s.at[3])
    table_ref[...] = have_s[:, share].reshape(levels, 128)
    column = lax.broadcasted_iota(jnp.int32, (levels, 128), 1)

    def mix_and_send(term):
        scale = jnp.sum(jnp.where(column == TERMS - 1 - term, table_ref[...], 0.0), axis=1, keepdims=True)
        for piece in range(share):
            mixed = full_product(m2l_ref[...], modes_ref[piece] * scale)
            for peer in range(slabs):
                give_g[peer, term, piece] = mixed[peer * 8 : peer * 8 + 8]
        for step in order2:
            peer = (slab + step) % slabs
            pltpu.make_async_remote_copy(
                src_ref=give_g.at[peer, term], dst_ref=have_g.at[term, slab],
                send_sem=sem_g.at[0, term], recv_sem=sem_g.at[1, term],
                device_id={"lev": peer}, device_id_type=MESH,
            ).start()
        have_g[term, slab] = give_g[slab, term]

    def wait_term(term, way):
        wait(have_g.at[term, pl.ds(0, slabs - 1)], sem_g.at[way, term])

    mix_and_send(0)
    mix_and_send(1)
    wait_term(0, 1)
    for tile in range(tiles):
        field[0, tile] = have_g[0, tile // share, tile % share]
        field[1, tile] = jnp.zeros((8, 128), jnp.float32)

    half = lax.broadcasted_iota(jnp.int32, (8, 128), 1) < 64
    bits = int(math.log2(tiles))

    def application(turn, carry):
        now = turn % 2
        old = 1 - now

        @pl.when(turn >= 2)
        def _():
            wait(send.at[now], sem_send.at[now])

        whole = [field[now, tile] for tile in range(tiles)]
        codes = [pack[place] for place in range(count)]
        for low, high in reversed(groups):
            for place in range(low, high):
                code = codes[place]
                lanes = code & 127
                found = [lane_gather(whole[tile], lanes) for tile in range(tiles)]
                for bit in range(bits):
                    odd = (code & (128 << bit)) != 0
                    found = [jnp.where(odd, found[2 * i + 1], found[2 * i]) for i in range(len(found) // 2)]
                send[now, place] = found[0]
            for place in range(low, high):
                pltpu.make_async_remote_copy(
                    src_ref=send.at[now, place], dst_ref=halo.at[now, inverse[place]],
                    send_sem=sem_send.at[now], recv_sem=sem_recv.at[now, groups.index((low, high))],
                    device_id={"cells": partition_at(place)}, device_id_type=MESH,
                ).start()

        @pl.when(turn + 2 < TERMS)
        def _():
            mix_and_send(turn + 2)

        for tile in range(tiles):
            g, t = tile // 8, tile % 8
            middle = field[now, tile]
            sides = jnp.where(half, field[now, min(tile + 1, tiles - 1)], field[now, max(tile - 1, 0)])
            value = middle * block(own[g, t : t + 1, :])
            for k in range(DEG):
                lanes = block(lane_a[k, g, t : t + 1, :])
                value = value + block(weight_a[k, g, t : t + 1, :]) * lane_gather(middle, lanes)
                value = value + block(weight_b[k, g, t : t + 1, :]) * lane_gather(sides, lanes)
            total[tile] = value

        @pl.when(turn == 0)
        def _():
            wait(flag_in, sem_flag.at[0])
            wait(flag_in, sem_flag.at[1])
            worst = flag_out[...]
            for place in range(count):
                worst = jnp.maximum(worst, flag_in[place])
            flag_ref[0, 0] = jnp.max(worst).astype(jnp.int32)

        wait_term(turn + 1, 1)
        scale = jnp.where(turn == TERMS - 2, 0.5, 1.0)
        extras = [zero] * spare
        for index, (low, high) in enumerate(groups):
            wait(halo.at[now, pl.ds(low, high - low)], sem_recv.at[now, index])
            last_group = index == len(groups) - 1
            for place in range(low, high):
                for slot in range(spare):
                    code = extra_code[slot]
                    got = lane_gather(halo[now, place], code & 127)
                    extras[slot] = jnp.where((code >> 7) == partition_at(place), got, extras[slot])
            for t in range(8):
                for group in range(group_count):
                    rows = range(group * group_rows, (group + 1) * group_rows)
                    values = [total[8 * g + t] for g in rows]
                    for place in range(low, high):
                        arrived = halo[now, place]
                        for r in range(rounds_of):
                            lanes = block(halo_lane[place, r, group, t : t + 1, :])
                            got = lane_gather(arrived, lanes)
                            for i, g in enumerate(rows):
                                values[i] = values[i] + block(halo_weight[place, r, g, t : t + 1, :]) * got
                    for i, g in enumerate(rows):
                        tile = 8 * g + t
                        if not last_group:
                            total[tile] = values[i]
                        else:
                            for slot in range(spare):
                                values[i] = values[i] + block(extra_weight[slot, g, t : t + 1, :]) * extras[slot]
                            field[old, tile] = (
                                have_g[turn + 1, tile // share, tile % share] + scale * values[i] - field[old, tile]
                            )
        return carry

    lax.fori_loop(0, TERMS - 1, application, 0)

    last = (TERMS - 1) % 2
    for tile in range(tiles):
        out_ref[:, tile * 128 : tile * 128 + 128] = field[last, tile]

    for now in range(2):
        wait(send.at[now], sem_send.at[now])
    wait(give_s.at[pl.ds(0, slabs - 1), pl.ds(0, share)], sem_s.at[0])
    wait(give_s.at[pl.ds(0, slabs - 1), share], sem_s.at[2])
    for term in range(TERMS):
        wait_term(term, 0)


def solve(parts, slabs, group_rows, rounds_of, spare, number, source, l2m, m2l, shift, weights, near, lists):
    columns = source.shape[1]
    tiles = columns // 128
    eighths = tiles // 8
    share = tiles // slabs
    peers = parts - 1
    f32, i32 = jnp.float32, jnp.int32
    groups = len(peers_of(parts // 2)[1])
    slots = max(spare, 1)
    return pl.pallas_call(
        functools.partial(kernel, parts, slabs, group_rows, rounds_of, spare),
        name=f"solve_{number}",
        out_shape=(
            jax.ShapeDtypeStruct(source.shape, f32),
            jax.ShapeDtypeStruct((1, 1), i32),
        ),
        in_specs=[pl.BlockSpec(memory_space=pltpu.HBM)] * 7,
        out_specs=(pl.BlockSpec(memory_space=pltpu.VMEM), pl.BlockSpec(memory_space=pltpu.SMEM)),
        scratch_shapes=[
            pltpu.VMEM(shift.shape, f32),
            pltpu.VMEM(source.shape, f32),
            pltpu.VMEM(l2m.shape, f32),
            pltpu.VMEM(m2l.shape, f32),
            pltpu.VMEM(weights.shape, f32),
            pltpu.VMEM(near.shape, i32),
            pltpu.VMEM(lists.shape, i32),
            pltpu.VMEM((DEG, eighths, 8, 128), i32),
            pltpu.VMEM((DEG, eighths, 8, 128), f32),
            pltpu.VMEM((DEG, eighths, 8, 128), i32),
            pltpu.VMEM((DEG, eighths, 8, 128), f32),
            pltpu.VMEM((DEG, eighths, 8, 128), f32),
            pltpu.VMEM((eighths, 8, 128), f32),
            pltpu.VMEM((peers, rounds_of, eighths // group_rows, 8, 128), i32),
            pltpu.VMEM((peers, rounds_of, eighths, 8, 128), f32),
            pltpu.VMEM((slots, 8, 128), i32),
            pltpu.VMEM((slots, eighths, 8, 128), f32),
            pltpu.VMEM((peers, 8, 128), i32),
            pltpu.VMEM((slabs, share + 1, 8, 128), f32),
            pltpu.VMEM((slabs, share + 1, 8, 128), f32),
            pltpu.VMEM((share, l2m.shape[0], 128), f32),
            pltpu.VMEM((l2m.shape[0], 128), f32),
            pltpu.VMEM((slabs, TERMS, share, 8, 128), f32),
            pltpu.VMEM((TERMS, slabs, share, 8, 128), f32),
            pltpu.VMEM((2, tiles, 8, 128), f32),
            pltpu.VMEM((tiles, 8, 128), f32),
            pltpu.VMEM((2, peers, 8, 128), f32),
            pltpu.VMEM((2, peers, 8, 128), f32),
            pltpu.VMEM((8, 128), f32),
            pltpu.VMEM((peers, 8, 128), f32),
            pltpu.SemaphoreType.DMA((7,)),
            pltpu.SemaphoreType.DMA((4,)),
            pltpu.SemaphoreType.DMA((2, TERMS)),
            pltpu.SemaphoreType.DMA((2,)),
            pltpu.SemaphoreType.DMA((2, groups)),
            pltpu.SemaphoreType.DMA((2,)),
        ],
        compiler_params=pltpu.CompilerParams(
            collective_id=number, has_side_effects=True, vmem_limit_bytes=40 << 20
        ),
    )(shift, source, l2m, m2l, weights, near, lists)


FAST = (4, 2, 3)
SAFE = (1, DEG, 0)


def solution(mesh):
    parts, slabs = mesh.shape["cells"], mesh.shape["lev"]

    def local(source, l2m, m2l, shift, weights, near, lists):
        arrays = (source, l2m, m2l, shift, weights, near, lists)
        eighths = source.shape[1] // 1024
        fast = (min(FAST[0], eighths), *FAST[1:])
        answer, flag = solve(parts, slabs, *fast, 0, *arrays)
        return lax.switch(
            flag[0, 0],
            (
                lambda arrays, answer: answer,
                lambda arrays, answer: solve(parts, slabs, *SAFE, 1, *arrays)[0],
            ),
            arrays,
            answer,
        )

    in_specs = (P("lev", "cells"), P(), P(), P("lev"), P(None, "cells"), P(None, "cells"), P("cells", None))
    return jax.shard_map(local, mesh=mesh, in_specs=in_specs, out_specs=P("lev", "cells"), check_vma=False)
```
